32 devices in a mesh: grp: 2 (over x), tok: 4 (over y, core), feat: 4 (over z).
Axes of the slice: x: 2, y: 2, z: 4, core: 2. Of those that a mesh axis runs over, the one named last changes fastest.
Arguments:
- activations: bfloat16 [4096, 3072], P(('grp', 'tok', 'feat')), parts along dimension 0, may hold values from -6 to 6
- block_lists: int32 [2048, 4], P(('grp', 'tok', 'feat')), parts along dimension 0, may hold values from 0 to 15, as said below
- top_positions: int32 [4096, 64], P(('grp', 'tok', 'feat')), parts along dimension 0, may hold values from 0 to 2047, as said below
- enc_weight: bfloat16 [3072, 8192], P(None, ('tok', 'feat')), may hold values from -0.109375 to 0.109375
- enc_bias: float32 [8192], P(('tok', 'feat')), may hold values from -3 to 3
- dec_weight: bfloat16 [8192, 3072], P(('tok', 'feat')), may hold values from -2.5 to 2.5
- dec_bias: float32 [3072], replicated, may hold values from -6 to 6
Outputs:
- enc_grad: bfloat16 [3072, 16384], P(None, ('grp', 'tok', 'feat')), parts along dimension 1
- dec_grad: bfloat16 [16384, 3072], P(('grp', 'tok', 'feat')), parts along dimension 0
The draws below stay inside these ranges and needn't reach their ends.
There are 2 independent parts, one for each index of `grp`. The reference program is written for one: setup_inputs(seed, part) draws one part's arguments, and reference() takes and returns one part's arrays. A program takes and returns all parts, laid end to end along the dimension named above; an argument that names none is the same for every part. Nothing has to cross between parts.
Inputs may be any that keep to these rules, and one draw needn't show every extreme that they name: `block_lists`: each row block names 4 different feature blocks. In the aligned blocks of 64 rows that one device holds, no feature block is named more than 24 times. In every draw one feature block is named exactly 24 times in every such block of rows. `top_positions`: the 64 entries of a token are distinct.
All inputs are finite; a program needn't handle non-finite values.
Results may differ from the reference program's by a relative error of at most 0.0058.
Values may be sent and summed in bfloat16 or wider, within the bound.
A program may use at most 128 MiB of HBM per device.

```python
import math
import jax
import jax.numpy as jnp
from jax import lax

D = 3072
BLOCK = 512
TOPK = 64
NACT = 4
RB = 2
OWNERS = 16
FEATURES = 8192
TOKENS = 2048
RB_DEV = 64
ROWBLOCKS = 1024
SLOTS = 24


def draw_block_lists(key, part):
    tickets = RB_DEV * NACT
    remain = tickets - SLOTS
    lowest = min(SLOTS, max(1, -(-remain // (OWNERS - 1))))
    base_order = jax.random.permutation(jax.random.fold_in(key, 1), OWNERS).astype(jnp.int32)
    hottest = base_order[0]
    others_all = base_order[1:]

    def one_device(dev_key):
        first_key, second_key, third_key, fourth_key = jax.random.split(dev_key, 4)
        shuffled = others_all[jax.random.permutation(first_key, OWNERS - 1)]
        run_length = jax.random.randint(second_key, (OWNERS - 1,), lowest, SLOTS + 1)
        run_ends = jnp.cumsum(run_length)
        ticket_spot = jnp.arange(remain, dtype=jnp.int32)
        run_number = jnp.sum((run_ends[None, :] <= ticket_spot[:, None]).astype(jnp.int32), axis=1)
        sequence = jnp.concatenate([jnp.full((SLOTS,), hottest, jnp.int32), shuffled[run_number].astype(jnp.int32)])
        table = sequence.reshape(NACT, RB_DEV).T
        table = table[jax.random.permutation(third_key, RB_DEV)]
        scores = jax.random.randint(fourth_key, (RB_DEV, NACT), 0, 1 << 20) * NACT + jnp.arange(NACT, dtype=jnp.int32)[None, :]
        col_order = jnp.argsort(scores, axis=1)
        return jnp.take_along_axis(table, col_order, axis=1)
    device_keys = jax.random.split(jax.random.fold_in(key, 2), OWNERS)
    return jax.vmap(one_device)(device_keys).reshape(ROWBLOCKS, NACT).astype(jnp.int32)


def draw_top_positions(key, part):
    candidates = NACT * BLOCK
    scores = jax.random.randint(jax.random.fold_in(key, 3), (TOKENS, candidates), 0, 1 << 16) * candidates + jnp.arange(candidates, dtype=jnp.int32)[None, :]
    return lax.top_k(scores, TOPK)[1].astype(jnp.int32)


def draw_dec_weight(key, part):
    first_key, second_key, third_key = jax.random.split(jax.random.fold_in(key, 4), 3)
    row_scale = jnp.exp(jax.random.uniform(first_key, (FEATURES, 1), jnp.float32) * math.log(10.0))
    col_scale = jnp.exp(jax.random.uniform(second_key, (1, D), jnp.float32) * math.log(10.0))
    entries = jnp.clip(jax.random.normal(third_key, (FEATURES, D), jnp.float32), -4.0, 4.0)
    return (entries * row_scale * col_scale / (20.0 * math.sqrt(TOPK))).astype(jnp.bfloat16)


def level_of(key, shape, cuts, low, top_value):
    level, own = 1.0, jax.random.fold_in(key, 6)
    for axis_at, parts in cuts:
        steps = jnp.exp(jax.random.uniform(jax.random.fold_in(own, axis_at), (parts,), jnp.float32, low / len(cuts), top_value / len(cuts)))
        level = level * jnp.repeat(steps, shape[axis_at] // parts).reshape([-1 if axis == axis_at else 1 for axis in range(len(shape))])
    return level


def normal_values(stream_key, dims, spread, limit, shards=(), held_as=jnp.bfloat16):
    values = spread * jax.random.normal(stream_key, dims, jnp.float32)
    if shards:
        values = values * level_of(stream_key, dims, shards, -0.22, 0.18)
    return jnp.clip(values, -limit, limit).astype(held_as)


def setup_inputs(seed: int = 0, part: int = 0) -> dict:
    streams_of = jax.random.split(jax.random.key(seed), 8)
    part_keys = jax.random.split(jax.random.fold_in(streams_of[7], part), 8)
    activations = normal_values(part_keys[0], (TOKENS, D), 1.0, 6.0, ((0, 16),))
    block_lists = draw_block_lists(jax.random.fold_in(jax.random.fold_in(streams_of[7], part), 71), part)
    top_positions = draw_top_positions(jax.random.fold_in(jax.random.fold_in(streams_of[7], part), 71), part)
    enc_weight = normal_values(streams_of[3], (D, FEATURES), D ** -0.5, 0.109375, ((1, 16),))
    enc_bias = normal_values(streams_of[4], (FEATURES,), 0.5, 3.0, ((0, 16),), jnp.float32)
    dec_weight = draw_dec_weight(jax.random.fold_in(streams_of[7], 71), part)
    dec_bias = normal_values(streams_of[6], (D,), 1.0, 6.0, (), jnp.float32)
    return dict(activations=activations, block_lists=block_lists, top_positions=top_positions, enc_weight=enc_weight, enc_bias=enc_bias, dec_weight=dec_weight, dec_bias=dec_bias)


def routed(owner, block_lists, top_positions):
    rowblock_total = block_lists.shape[0]
    hit_table = (block_lists == owner).astype(jnp.int32)
    member_flag = jnp.sum(hit_table, axis=1).astype(jnp.int32)
    column_index = jnp.argmax(hit_table, axis=1).astype(jnp.int32)
    order_key = (1 - member_flag) * rowblock_total + jnp.arange(rowblock_total, dtype=jnp.int32)
    picked = jnp.argsort(order_key)[: OWNERS * SLOTS].astype(jnp.int32)
    lane_index = jnp.arange(RB, dtype=jnp.int32)
    row_index = (picked[:, None] * RB + lane_index[None, :]).reshape(-1).astype(jnp.int32)
    block_cols = jnp.repeat(column_index[picked], RB)
    valid_flag = jnp.repeat(member_flag[picked], RB)
    offsets = top_positions[row_index] - block_cols[:, None] * BLOCK
    inside = (offsets >= 0) & (offsets < BLOCK) & (valid_flag[:, None] > 0)
    offsets = jnp.where(inside, offsets, BLOCK).astype(jnp.int32)
    slot_total = row_index.shape[0]
    line_index = jnp.arange(slot_total, dtype=jnp.int32)[:, None]
    feat_mask = jnp.zeros((slot_total, BLOCK), jnp.float32).at[line_index, offsets].set(1.0, mode="drop")
    return row_index, feat_mask


def encode(owner, activations, block_lists, top_positions, enc_weight, enc_bias):
    row_index, feat_mask = routed(owner, block_lists, top_positions)
    start = (owner * BLOCK).astype(jnp.int32)
    enc_cols = lax.dynamic_slice_in_dim(enc_weight, start, BLOCK, 1)
    bias_part = lax.dynamic_slice_in_dim(enc_bias, start, BLOCK, 0)
    picked_rows = activations[row_index]
    pre_acts = jnp.dot(picked_rows, enc_cols, preferred_element_type=jnp.float32) + bias_part
    code_vals = (feat_mask * pre_acts).astype(jnp.bfloat16)
    return row_index, feat_mask, picked_rows, code_vals, start


def reference(activations, block_lists, top_positions, enc_weight, enc_bias, dec_weight, dec_bias):
    def add_partial(owner, recon):
        row_index, feat_mask, picked_rows, code_vals, start = encode(owner, activations, block_lists, top_positions, enc_weight, enc_bias)
        dec_rows = lax.dynamic_slice_in_dim(dec_weight, start, BLOCK, 0)
        partial_value = jnp.dot(code_vals, dec_rows, preferred_element_type=jnp.float32).astype(jnp.bfloat16)
        return recon.at[row_index].add(partial_value.astype(jnp.float32))

    recon = lax.fori_loop(0, OWNERS, add_partial, jnp.zeros((TOKENS, D), jnp.float32))
    residual = (recon + dec_bias - activations.astype(jnp.float32)).astype(jnp.bfloat16)

    def gradients(owner):
        row_index, feat_mask, picked_rows, code_vals, start = encode(owner, activations, block_lists, top_positions, enc_weight, enc_bias)
        dec_rows = lax.dynamic_slice_in_dim(dec_weight, start, BLOCK, 0)
        picked_err = residual[row_index]
        grad_codes = lax.dot_general(picked_err, dec_rows, (((1,), (1,)), ((), ())), preferred_element_type=jnp.float32)
        grad_pre = (feat_mask * grad_codes).astype(jnp.bfloat16)
        enc_part = lax.dot_general(picked_rows, grad_pre, (((0,), (0,)), ((), ())), preferred_element_type=jnp.float32).astype(jnp.bfloat16)
        raw_grad = lax.dot_general(code_vals, picked_err, (((0,), (0,)), ((), ())), preferred_element_type=jnp.float32)
        dec_float = dec_rows.astype(jnp.float32)
        along_coef = jnp.sum(raw_grad * dec_float, axis=1) / (jnp.sum(dec_float * dec_float, axis=1) + 1e-6)
        dec_part = (raw_grad - along_coef[:, None] * dec_float).astype(jnp.bfloat16)
        return enc_part, dec_part

    enc_stack, dec_stack = lax.map(gradients, jnp.arange(OWNERS, dtype=jnp.int32))
    enc_grad = jnp.transpose(enc_stack, (1, 0, 2)).reshape(D, FEATURES)
    dec_grad = dec_stack.reshape(FEATURES, D)
    return (enc_grad, dec_grad)
```

```python
import jax
import jax.numpy as jnp
from jax import lax
from jax.sharding import PartitionSpec as P


def dispatch_rows(send_x, send_rel):
    result = (
        lax.all_to_all(send_x, ("tok", "feat"), split_axis=0, concat_axis=0, tiled=True),
        lax.all_to_all(send_rel, ("tok", "feat"), split_axis=0, concat_axis=0, tiled=True),
    )
    return result


def return_partials(partial_value):
    result = lax.all_to_all(partial_value, ("tok", "feat"), split_axis=0, concat_axis=0, tiled=True)
    return result


def dispatch_errors(send_err):
    result = lax.all_to_all(send_err, ("tok", "feat"), split_axis=0, concat_axis=0, tiled=True)
    return result


def routed_plan(activations, block_lists, top_positions, enc_weight, enc_bias, dec_weight, dec_bias):
    owner_count = lax.axis_size(("tok", "feat"))
    token_count, model_width = activations.shape
    block_rows, active_count = block_lists.shape
    group_rows = token_count // block_rows
    feat_block = enc_weight.shape[1]
    top_count = top_positions.shape[1]
    slot_count = max(2, 3 * token_count * active_count // (2 * group_rows * owner_count))
    per_owner = slot_count * group_rows
    buffer_rows = owner_count * per_owner
    pair_count = block_rows * active_count
    pair_ids = block_lists.reshape(pair_count)
    pair_order = jnp.arange(pair_count, dtype=jnp.int32)
    earlier = (pair_ids[:, None] == pair_ids[None, :]) & (pair_order[None, :] < pair_order[:, None])
    pair_rank = jnp.sum(earlier.astype(jnp.int32), axis=1)
    lane_index = jnp.arange(group_rows, dtype=jnp.int32)
    target = (
        (pair_ids * per_owner + pair_rank * group_rows)[:, None] + lane_index[None, :]
    ).reshape(-1)
    source = ((pair_order // active_count * group_rows)[:, None] + lane_index[None, :]).reshape(-1)
    column = jnp.repeat(pair_order % active_count, group_rows)
    slot_index = jnp.arange(buffer_rows, dtype=jnp.int32)
    hit_bool = slot_index[:, None] == target[None, :]
    hit_float = hit_bool.astype(jnp.float32)
    place_float = jnp.sum(
        hit_float.reshape(buffer_rows, block_rows, active_count, group_rows), axis=2
    ).reshape(buffer_rows, token_count)
    place = place_float.astype(jnp.bfloat16)
    filled = jnp.sum(place_float, axis=1)
    send_x = jnp.dot(place, activations, preferred_element_type=jnp.float32).astype(jnp.bfloat16)
    offsets = top_positions[source] - column[:, None] * feat_block
    offsets = jnp.where((offsets >= 0) & (offsets < feat_block), offsets, feat_block)
    rel_float = (
        jnp.dot(hit_float, offsets.astype(jnp.float32), precision=lax.Precision.HIGHEST)
        + (1.0 - filled)[:, None] * feat_block
    )
    send_rel = rel_float.astype(jnp.int32)
    recv_x, recv_rel = dispatch_rows(
        send_x.reshape(owner_count, per_owner, model_width),
        send_rel.reshape(owner_count, per_owner, top_count),
    )
    recv_x = recv_x.reshape(buffer_rows, model_width)
    recv_rel = recv_rel.reshape(buffer_rows, top_count)
    feature_iota = jnp.arange(feat_block, dtype=jnp.int32)
    mask_bool = jnp.zeros((buffer_rows, feat_block), jnp.bool_)
    for begin in range(0, top_count, 8):
        piece = recv_rel[:, begin : begin + 8]
        mask_bool = mask_bool | jnp.any(piece[:, :, None] == feature_iota[None, None, :], axis=1)
    feat_mask = mask_bool.astype(jnp.float32)
    pre_acts = jnp.dot(recv_x, enc_weight, preferred_element_type=jnp.float32) + enc_bias
    code_vals = (feat_mask * pre_acts).astype(jnp.bfloat16)
    partial_value = jnp.dot(code_vals, dec_weight, preferred_element_type=jnp.float32).astype(
        jnp.bfloat16
    )
    returned = return_partials(partial_value.reshape(owner_count, per_owner, model_width)).reshape(
        buffer_rows, model_width
    )
    summed = lax.dot_general(
        place, returned, (((0,), (0,)), ((), ())), preferred_element_type=jnp.float32
    )
    residual = (summed + dec_bias - activations.astype(jnp.float32)).astype(jnp.bfloat16)
    send_err = jnp.dot(place, residual, preferred_element_type=jnp.float32).astype(jnp.bfloat16)
    recv_err = dispatch_errors(send_err.reshape(owner_count, per_owner, model_width)).reshape(
        buffer_rows, model_width
    )
    grad_codes = lax.dot_general(
        recv_err, dec_weight, (((1,), (1,)), ((), ())), preferred_element_type=jnp.float32
    )
    grad_pre = (feat_mask * grad_codes).astype(jnp.bfloat16)
    enc_grad = lax.dot_general(
        recv_x, grad_pre, (((0,), (0,)), ((), ())), preferred_element_type=jnp.float32
    ).astype(jnp.bfloat16)
    raw_grad = lax.dot_general(
        code_vals, recv_err, (((0,), (0,)), ((), ())), preferred_element_type=jnp.float32
    )
    dec_float = dec_weight.astype(jnp.float32)
    along_coef = jnp.sum(raw_grad * dec_float, axis=1) / (
        jnp.sum(dec_float * dec_float, axis=1) + 1e-06
    )
    dec_grad = (raw_grad - along_coef[:, None] * dec_float).astype(jnp.bfloat16)
    return (enc_grad, dec_grad)


GROUP = ("tok", "feat")


def global_ids(block_lists, top_positions, feat_block):
    token_count = top_positions.shape[0]
    block_rows, active_count = block_lists.shape
    lists = jnp.repeat(block_lists, token_count // block_rows, axis=0)
    column = top_positions // feat_block
    chosen = jnp.zeros_like(top_positions)
    for k in range(active_count):
        chosen = jnp.where(column == k, lists[:, k : k + 1], chosen)
    return chosen * feat_block + top_positions % feat_block


def select_mask(rel, feat_block):
    words = feat_block // 8
    inside = (rel >= 0) & (rel < feat_block)
    word = jnp.where(inside, rel // 8, words)
    bit = jnp.left_shift(1, rel & 7)
    word_iota = jnp.arange(words, dtype=jnp.int32)
    packed = jnp.sum(
        jnp.where(word[:, :, None] == word_iota[None, None, :], bit[:, :, None], 0), axis=1
    )
    feature_iota = jnp.arange(feat_block, dtype=jnp.int32)
    spread = (word_iota[:, None] == (feature_iota // 8)[None, :]).astype(jnp.bfloat16)
    wide = jnp.dot(
        packed.astype(jnp.float32).astype(jnp.bfloat16), spread, preferred_element_type=jnp.float32
    ).astype(jnp.int32)
    return (jnp.right_shift(wide, (feature_iota & 7)[None, :]) & 1).astype(jnp.bfloat16)


def gathered_plan(activations, block_lists, top_positions, enc_weight, enc_bias, dec_weight, dec_bias):
    feat_block = enc_weight.shape[1]
    ids = global_ids(block_lists, top_positions, feat_block)
    all_ids = lax.all_gather(ids, GROUP, axis=0, tiled=True)
    all_x = lax.all_gather(activations, GROUP, axis=0, tiled=True)
    mask = select_mask(all_ids - lax.axis_index(GROUP) * feat_block, feat_block)
    pre_acts = jnp.dot(all_x, enc_weight, preferred_element_type=jnp.float32) + enc_bias
    code_vals = jnp.where(mask > 0, pre_acts, 0.0).astype(jnp.bfloat16)
    partial_value = jnp.dot(code_vals, dec_weight, preferred_element_type=jnp.float32).astype(
        jnp.bfloat16
    )
    summed = lax.psum_scatter(partial_value, GROUP, scatter_dimension=0, tiled=True)
    residual = (
        summed.astype(jnp.float32) + dec_bias - activations.astype(jnp.float32)
    ).astype(jnp.bfloat16)
    all_err = lax.all_gather(residual, GROUP, axis=0, tiled=True)
    grad_codes = lax.dot_general(
        all_err, dec_weight, (((1,), (1,)), ((), ())), preferred_element_type=jnp.float32
    )
    grad_pre = jnp.where(mask > 0, grad_codes, 0.0).astype(jnp.bfloat16)
    enc_grad = lax.dot_general(
        all_x, grad_pre, (((0,), (0,)), ((), ())), preferred_element_type=jnp.float32
    ).astype(jnp.bfloat16)
    raw_grad = lax.dot_general(
        code_vals, all_err, (((0,), (0,)), ((), ())), preferred_element_type=jnp.float32
    )
    dec_float = dec_weight.astype(jnp.float32)
    along_coef = jnp.sum(raw_grad * dec_float, axis=1) / (
        jnp.sum(dec_float * dec_float, axis=1) + 1e-06
    )
    dec_grad = (raw_grad - along_coef[:, None] * dec_float).astype(jnp.bfloat16)
    return (enc_grad, dec_grad)


def on_device(activations, block_lists, top_positions, *weights):
    owner_count = lax.axis_size(GROUP)
    pairs = activations.shape[0] * block_lists.shape[1]
    gathered = owner_count * activations.shape[0]
    if gathered <= 4 * pairs:
        return gathered_plan(activations, block_lists, top_positions, *weights)
    return routed_plan(activations, block_lists, top_positions, *weights)


def solution(mesh):
    placed = (
        P(("grp", "tok", "feat"), None),
        P(("grp", "tok", "feat"), None),
        P(("grp", "tok", "feat"), None),
        P(None, ("tok", "feat")),
        P(("tok", "feat")),
        P(("tok", "feat"), None),
        P(),
    )
    return jax.shard_map(
        on_device,
        mesh=mesh,
        in_specs=placed,
        out_specs=(P(None, ("grp", "tok", "feat")), P(("grp", "tok", "feat"), None)),
        check_vma=False,
    )
```

```python
import functools

import jax
import jax.numpy as jnp
from jax import lax
from jax.experimental import pallas as pl
from jax.experimental.pallas import tpu as pltpu
from jax.sharding import PartitionSpec as P


def dispatch_rows(send_x, send_rel):
    result = (
        lax.all_to_all(send_x, ("tok", "feat"), split_axis=0, concat_axis=0, tiled=True),
        lax.all_to_all(send_rel, ("tok", "feat"), split_axis=0, concat_axis=0, tiled=True),
    )
    return result


def return_partials(partial_value):
    result = lax.all_to_all(partial_value, ("tok", "feat"), split_axis=0, concat_axis=0, tiled=True)
    return result


def dispatch_errors(send_err):
    result = lax.all_to_all(send_err, ("tok", "feat"), split_axis=0, concat_axis=0, tiled=True)
    return result


def routed_plan(activations, block_lists, top_positions, enc_weight, enc_bias, dec_weight, dec_bias):
    owner_count = lax.axis_size(("tok", "feat"))
    token_count, model_width = activations.shape
    block_rows, active_count = block_lists.shape
    group_rows = token_count // block_rows
    feat_block = enc_weight.shape[1]
    top_count = top_positions.shape[1]
    slot_count = max(2, 3 * token_count * active_count // (2 * group_rows * owner_count))
    per_owner = slot_count * group_rows
    buffer_rows = owner_count * per_owner
    pair_count = block_rows * active_count
    pair_ids = block_lists.reshape(pair_count)
    pair_order = jnp.arange(pair_count, dtype=jnp.int32)
    earlier = (pair_ids[:, None] == pair_ids[None, :]) & (pair_order[None, :] < pair_order[:, None])
    pair_rank = jnp.sum(earlier.astype(jnp.int32), axis=1)
    lane_index = jnp.arange(group_rows, dtype=jnp.int32)
    target = (
        (pair_ids * per_owner + pair_rank * group_rows)[:, None] + lane_index[None, :]
    ).reshape(-1)
    source = ((pair_order // active_count * group_rows)[:, None] + lane_index[None, :]).reshape(-1)
    column = jnp.repeat(pair_order % active_count, group_rows)
    slot_index = jnp.arange(buffer_rows, dtype=jnp.int32)
    hit_bool = slot_index[:, None] == target[None, :]
    hit_float = hit_bool.astype(jnp.float32)
    place_float = jnp.sum(
        hit_float.reshape(buffer_rows, block_rows, active_count, group_rows), axis=2
    ).reshape(buffer_rows, token_count)
    place = place_float.astype(jnp.bfloat16)
    filled = jnp.sum(place_float, axis=1)
    send_x = jnp.dot(place, activations, preferred_element_type=jnp.float32).astype(jnp.bfloat16)
    offsets = top_positions[source] - column[:, None] * feat_block
    offsets = jnp.where((offsets >= 0) & (offsets < feat_block), offsets, feat_block)
    rel_float = (
        jnp.dot(hit_float, offsets.astype(jnp.float32), precision=lax.Precision.HIGHEST)
        + (1.0 - filled)[:, None] * feat_block
    )
    send_rel = rel_float.astype(jnp.int32)
    recv_x, recv_rel = dispatch_rows(
        send_x.reshape(owner_count, per_owner, model_width),
        send_rel.reshape(owner_count, per_owner, top_count),
    )
    recv_x = recv_x.reshape(buffer_rows, model_width)
    recv_rel = recv_rel.reshape(buffer_rows, top_count)
    feature_iota = jnp.arange(feat_block, dtype=jnp.int32)
    mask_bool = jnp.zeros((buffer_rows, feat_block), jnp.bool_)
    for begin in range(0, top_count, 8):
        piece = recv_rel[:, begin : begin + 8]
        mask_bool = mask_bool | jnp.any(piece[:, :, None] == feature_iota[None, None, :], axis=1)
    feat_mask = mask_bool.astype(jnp.float32)
    pre_acts = jnp.dot(recv_x, enc_weight, preferred_element_type=jnp.float32) + enc_bias
    code_vals = (feat_mask * pre_acts).astype(jnp.bfloat16)
    partial_value = jnp.dot(code_vals, dec_weight, preferred_element_type=jnp.float32).astype(
        jnp.bfloat16
    )
    returned = return_partials(partial_value.reshape(owner_count, per_owner, model_width)).reshape(
        buffer_rows, model_width
    )
    summed = lax.dot_general(
        place, returned, (((0,), (0,)), ((), ())), preferred_element_type=jnp.float32
    )
    residual = (summed + dec_bias - activations.astype(jnp.float32)).astype(jnp.bfloat16)
    send_err = jnp.dot(place, residual, preferred_element_type=jnp.float32).astype(jnp.bfloat16)
    recv_err = dispatch_errors(send_err.reshape(owner_count, per_owner, model_width)).reshape(
        buffer_rows, model_width
    )
    grad_codes = lax.dot_general(
        recv_err, dec_weight, (((1,), (1,)), ((), ())), preferred_element_type=jnp.float32
    )
    grad_pre = (feat_mask * grad_codes).astype(jnp.bfloat16)
    enc_grad = lax.dot_general(
        recv_x, grad_pre, (((0,), (0,)), ((), ())), preferred_element_type=jnp.float32
    ).astype(jnp.bfloat16)
    raw_grad = lax.dot_general(
        code_vals, recv_err, (((0,), (0,)), ((), ())), preferred_element_type=jnp.float32
    )
    dec_float = dec_weight.astype(jnp.float32)
    along_coef = jnp.sum(raw_grad * dec_float, axis=1) / (
        jnp.sum(dec_float * dec_float, axis=1) + 1e-06
    )
    dec_grad = (raw_grad - along_coef[:, None] * dec_float).astype(jnp.bfloat16)
    return (enc_grad, dec_grad)


GROUP = ("tok", "feat")


def global_ids(block_lists, top_positions, feat_block):
    token_count = top_positions.shape[0]
    block_rows, active_count = block_lists.shape
    lists = jnp.repeat(block_lists, token_count // block_rows, axis=0)
    column = top_positions // feat_block
    chosen = jnp.zeros_like(top_positions)
    for k in range(active_count):
        chosen = jnp.where(column == k, lists[:, k : k + 1], chosen)
    return chosen * feat_block + top_positions % feat_block


def select_mask(rel, feat_block):
    words = feat_block // 8
    inside = (rel >= 0) & (rel < feat_block)
    word = jnp.where(inside, rel // 8, words)
    bit = jnp.left_shift(1, rel & 7)
    word_iota = jnp.arange(words, dtype=jnp.int32)
    packed = jnp.sum(
        jnp.where(word[:, :, None] == word_iota[None, None, :], bit[:, :, None], 0), axis=1
    )
    feature_iota = jnp.arange(feat_block, dtype=jnp.int32)
    spread = (word_iota[:, None] == (feature_iota // 8)[None, :]).astype(jnp.bfloat16)
    wide = jnp.dot(
        packed.astype(jnp.float32).astype(jnp.bfloat16), spread, preferred_element_type=jnp.float32
    ).astype(jnp.int32)
    return (jnp.right_shift(wide, (feature_iota & 7)[None, :]) & 1).astype(jnp.bfloat16)


MESH = pl.DeviceIdType.MESH


def place_in_group(zs):
    tok, z = lax.axis_index("tok"), lax.axis_index("feat")
    y, core = tok // 2, tok % 2
    links = {
        "core": {"tok": y * 2 + (1 - core)},
        "y": {"tok": (1 - y) * 2 + core},
        "up": {"feat": jnp.minimum(z + 1, zs - 1)},
        "down": {"feat": jnp.maximum(z - 1, 0)},
    }
    return y, core, z, links


def greet(z, zs, links):
    barrier = pltpu.get_barrier_semaphore()
    for kind in ("core", "y"):
        pl.semaphore_signal(barrier, inc=1, device_id=links[kind], device_id_type=MESH)

    @pl.when(z < zs - 1)
    def _():
        pl.semaphore_signal(barrier, inc=1, device_id=links["up"], device_id_type=MESH)

    @pl.when(z > 0)
    def _():
        pl.semaphore_signal(barrier, inc=1, device_id=links["down"], device_id_type=MESH)

    pl.semaphore_wait(barrier, 2 + jnp.minimum(z, 1) + jnp.minimum(zs - 1 - z, 1))


KINDS = ("up", "down", "y", "core")


def gather_kernel(zs, splits, *refs):
    count = len(splits)
    sources, gathered = refs[:count], refs[count : 2 * count]
    send, recv, own = refs[2 * count :]
    y, core, z, links = place_in_group(zs)
    pieces = [(a, p) for a in range(count) for p in range(splits[a])]

    def block(yy, cc, zz):
        return (yy * 2 + cc) * zs + zz

    mine = block(y, core, z)

    def rows_of(a, p, b):
        step = sources[a].shape[0] // splits[a]
        return gathered[a].at[pl.ds(b * sources[a].shape[0] + p * step, step)]

    def copy(kind, i, b, from_source=False):
        a, p = pieces[i]
        step = sources[a].shape[0] // splits[a]
        rows = rows_of(a, p, b)
        return pltpu.make_async_remote_copy(
            src_ref=sources[a].at[pl.ds(p * step, step)] if from_source else rows,
            dst_ref=rows,
            send_sem=send.at[KINDS.index(kind), b, i],
            recv_sem=recv.at[b, i],
            device_id=links[kind],
            device_id_type=MESH,
        )

    greet(z, zs, links)
    kept = []
    for a in range(count):
        total = sources[a].shape[0]
        kept.append(
            pltpu.make_async_copy(
                sources[a], gathered[a].at[pl.ds(mine * total, total)], own.at[a]
            )
        )
        kept[-1].start()
    order = list(range(len(pieces)))
    for i in order:

        @pl.when(z < zs - 1)
        def _():
            copy("up", i, mine, True).start()

        @pl.when(z > 0)
        def _():
            copy("down", i, mine, True).start()

        copy("y", i, mine, True).start()
        copy("core", i, mine, True).start()

    def at_distance(d):
        if d == 0:
            return [(None, z, None, None)]
        return [
            (z - d >= 0, z - d, "up", z < zs - 1),
            (z + d < zs, z + d, "down", z > 0),
        ]

    for d in range(1, zs + 1):
        for i in order:
            if d < zs:
                for valid, zz, kind, onward in at_distance(d):

                    @pl.when(valid)
                    def _():
                        b = block(y, core, zz)
                        copy("core", i, b).wait_recv()

                        @pl.when(onward)
                        def _():
                            copy(kind, i, b).start()

                        copy("y", i, b).start()
                        copy("core", i, b).start()

            for valid, zz, kind, onward in at_distance(d - 1):

                def pass_on():
                    b = block(1 - y, core, zz)
                    copy("core", i, b).wait_recv()
                    copy("core", i, b).start()

                if valid is None:
                    pass_on()
                else:
                    pl.when(valid)(pass_on)
    for i in order:
        for yy in range(2):
            for zz in range(zs):
                b = block(yy, 1 - core, zz)
                copy("core", i, b).wait_recv()
    for a in range(count):
        kept[a].wait()
    for i in order:

        @pl.when(z < zs - 1)
        def _():
            copy("up", i, mine, True).wait_send()

        @pl.when(z > 0)
        def _():
            copy("down", i, mine, True).wait_send()

        copy("y", i, mine, True).wait_send()
        copy("core", i, mine, True).wait_send()
        for d in range(1, zs):
            for valid, zz, kind, onward in at_distance(d):

                @pl.when(valid)
                def _():
                    b = block(y, core, zz)

                    @pl.when(onward)
                    def _():
                        copy(kind, i, b).wait_send()

                    copy("y", i, b).wait_send()
                    copy("core", i, b).wait_send()

        for zz in range(zs):
            copy("core", i, block(1 - y, core, zz)).wait_send()


def gather_rows(arrays, splits, collective_id):
    owner_count, zs = lax.axis_size(GROUP), lax.axis_size("feat")
    count = sum(splits)
    return pl.pallas_call(
        functools.partial(gather_kernel, zs, splits),
        out_shape=[
            jax.ShapeDtypeStruct((owner_count * a.shape[0],) + a.shape[1:], a.dtype) for a in arrays
        ],
        in_specs=[pl.BlockSpec(memory_space=pl.ANY)] * len(arrays),
        out_specs=[pl.BlockSpec(memory_space=pl.ANY)] * len(arrays),
        scratch_shapes=[
            pltpu.SemaphoreType.DMA((len(KINDS), owner_count, count)),
            pltpu.SemaphoreType.DMA((owner_count, count)),
            pltpu.SemaphoreType.DMA((len(arrays),)),
        ],
        compiler_params=pltpu.CompilerParams(collective_id=collective_id, has_side_effects=True),
        name="gather_rows",
    )(*arrays)


def reduce_kernel(
    zs, x_ref, bias_ref, codes_ref, dec_ref, out_ref,
    a_out, a_in, b_out, b_in, c_out, c_in, a_send, a_recv, b_send, b_recv, c_send, c_recv,
):
    y, core, z, links = place_in_group(zs)
    rows, width = out_ref.shape
    tile = 768

    def product(yy, cc, zz, added, write):
        begin = pl.multiple_of(((yy * 2 + cc) * zs + zz) * rows, rows)

        def body(j, carry):
            cols = pl.ds(pl.multiple_of(j * tile, tile), tile)
            acc = jnp.dot(
                codes_ref[pl.ds(begin, rows), :], dec_ref[:, cols],
                preferred_element_type=jnp.float32,
            )
            for read in added:
                acc += read(cols).astype(jnp.float32)
            write(cols, acc)
            return carry

        lax.fori_loop(0, width // tile, body, 0)

    def store_at(ref, slot):
        def write(cols, acc):
            ref[slot, :, cols] = acc.astype(jnp.bfloat16)

        return write

    def load_at(ref, *slot):
        return lambda cols: ref[(*slot, slice(None), cols)]

    def copy_a(slot):
        return pltpu.make_async_remote_copy(
            src_ref=a_out.at[slot], dst_ref=a_in.at[slot], send_sem=a_send.at[slot],
            recv_sem=a_recv.at[slot], device_id=links["core"], device_id_type=MESH,
        )

    def copy_b(zz):
        return pltpu.make_async_remote_copy(
            src_ref=b_out.at[zz], dst_ref=b_in.at[zz], send_sem=b_send.at[zz],
            recv_sem=b_recv.at[zz], device_id=links["y"], device_id_type=MESH,
        )

    def copy_c(way, zz):
        return pltpu.make_async_remote_copy(
            src_ref=c_out.at[zz], dst_ref=c_in.at[way, zz], send_sem=c_send.at[zz],
            recv_sem=c_recv.at[way, zz], device_id=links["up" if way == 0 else "down"],
            device_id_type=MESH,
        )

    rounds = []
    for d in range(zs - 1, 0, -1):
        rounds.append((z + d < zs, z + d, 0))
        rounds.append((z - d >= 0, z - d, 1))
    rounds.append((None, z, None))

    def run(valid, action):
        if valid is None:
            action()
        else:
            pl.when(valid)(action)

    greet(z, zs, links)
    for valid, zz, way in rounds:

        def pair_step():
            for yy in (1 - y, y):
                slot = yy * zs + zz
                product(yy, 1 - core, zz, (), store_at(a_out, slot))
                copy_a(slot).start()
            slot = (1 - y) * zs + zz
            copy_a(slot).wait_recv()
            product(1 - y, core, zz, (load_at(a_in, slot),), store_at(b_out, zz))
            copy_b(zz).start()

        run(valid, pair_step)
    for valid, zz, way in rounds[:-1]:
        first = (z == 0) if way == 0 else (z == zs - 1)

        def line_step():
            slot = y * zs + zz
            copy_a(slot).wait_recv()
            copy_b(zz).wait_recv()
            near = (load_at(a_in, slot), load_at(b_in, zz))

            @pl.when(first)
            def _():
                product(y, core, zz, near, store_at(c_out, zz))

            @pl.when(jnp.logical_not(first))
            def _():
                copy_c(way, zz).wait_recv()
                product(y, core, zz, near + (load_at(c_in, way, zz),), store_at(c_out, zz))

            copy_c(way, zz).start()

        run(valid, line_step)
    slot = y * zs + z
    copy_a(slot).wait_recv()
    copy_b(z).wait_recv()

    def finish(cols, acc):
        out_ref[:, cols] = (
            acc + bias_ref[:, cols] - x_ref[:, cols].astype(jnp.float32)
        ).astype(jnp.bfloat16)

    near = (load_at(a_in, slot), load_at(b_in, z))

    @pl.when(z == 0)
    def _():
        copy_c(1, z).wait_recv()
        product(y, core, z, near + (load_at(c_in, 1, z),), finish)

    @pl.when(z == zs - 1)
    def _():
        copy_c(0, z).wait_recv()
        product(y, core, z, near + (load_at(c_in, 0, z),), finish)

    @pl.when((z > 0) & (z < zs - 1))
    def _():
        copy_c(1, z).wait_recv()
        copy_c(0, z).wait_recv()
        product(y, core, z, near + (load_at(c_in, 0, z), load_at(c_in, 1, z)), finish)

    for slot in range(2 * zs):
        copy_a(slot).wait_send()
    for zz in range(zs):
        copy_b(zz).wait_send()
    for valid, zz, way in rounds[:-1]:
        run(valid, lambda: copy_c(way, zz).wait_send())


def reduce_rows(x, bias, codes, dec_weight, collective_id):
    zs = lax.axis_size("feat")
    rows, width = x.shape
    slab = lambda *lead: pltpu.VMEM(lead + (rows, width), jnp.bfloat16)
    sem = lambda *lead: pltpu.SemaphoreType.DMA(lead)
    return pl.pallas_call(
        functools.partial(reduce_kernel, zs),
        out_shape=jax.ShapeDtypeStruct((rows, width), jnp.bfloat16),
        in_specs=[pl.BlockSpec(memory_space=pltpu.VMEM)] * 4,
        out_specs=pl.BlockSpec(memory_space=pltpu.VMEM),
        scratch_shapes=[
            slab(2 * zs), slab(2 * zs), slab(zs), slab(zs), slab(zs), slab(2, zs),
            sem(2 * zs), sem(2 * zs), sem(zs), sem(zs), sem(zs), sem(2, zs),
        ],
        compiler_params=pltpu.CompilerParams(
            collective_id=collective_id, has_side_effects=True, vmem_limit_bytes=48 * 1024 * 1024
        ),
        name="reduce_rows",
    )(x, bias.reshape(1, width), codes, dec_weight)


def gathered_plan(activations, block_lists, top_positions, enc_weight, enc_bias, dec_weight, dec_bias):
    feat_block = enc_weight.shape[1]
    ids = global_ids(block_lists, top_positions, feat_block)
    all_ids, all_x = gather_rows([ids, activations], (1, 2), 1)
    mask = select_mask(all_ids - lax.axis_index(GROUP) * feat_block, feat_block)
    pre_acts = jnp.dot(all_x, enc_weight, preferred_element_type=jnp.float32) + enc_bias
    code_vals = jnp.where(mask > 0, pre_acts, 0.0).astype(jnp.bfloat16)
    residual = reduce_rows(activations, dec_bias, code_vals, dec_weight, 2)
    (all_err,) = gather_rows([residual], (2,), 3)
    grad_codes = lax.dot_general(
        all_err, dec_weight, (((1,), (1,)), ((), ())), preferred_element_type=jnp.float32
    )
    grad_pre = jnp.where(mask > 0, grad_codes, 0.0).astype(jnp.bfloat16)
    enc_grad = lax.dot_general(
        all_x, grad_pre, (((0,), (0,)), ((), ())), preferred_element_type=jnp.float32
    ).astype(jnp.bfloat16)
    raw_grad = lax.dot_general(
        code_vals, all_err, (((0,), (0,)), ((), ())), preferred_element_type=jnp.float32
    )
    dec_float = dec_weight.astype(jnp.float32)
    along_coef = jnp.sum(raw_grad * dec_float, axis=1) / (
        jnp.sum(dec_float * dec_float, axis=1) + 1e-06
    )
    dec_grad = (raw_grad - along_coef[:, None] * dec_float).astype(jnp.bfloat16)
    return (enc_grad, dec_grad)


def on_device(activations, block_lists, top_positions, *weights):
    owner_count = lax.axis_size(GROUP)
    pairs = activations.shape[0] * block_lists.shape[1]
    gathered = owner_count * activations.shape[0]
    square = lax.axis_size("tok") == 4 and activations.shape[1] % 768 == 0
    if square and gathered <= 4 * pairs:
        return gathered_plan(activations, block_lists, top_positions, *weights)
    return routed_plan(activations, block_lists, top_positions, *weights)


def solution(mesh):
    placed = (
        P(("grp", "tok", "feat"), None),
        P(("grp", "tok", "feat"), None),
        P(("grp", "tok", "feat"), None),
        P(None, ("tok", "feat")),
        P(("tok", "feat")),
        P(("tok", "feat"), None),
        P(),
    )
    return jax.shard_map(
        on_device,
        mesh=mesh,
        in_specs=placed,
        out_specs=(P(None, ("grp", "tok", "feat")), P(("grp", "tok", "feat"), None)),
        check_vma=False,
    )
```

```python
import functools

import jax
import jax.numpy as jnp
from jax import lax
from jax.experimental import pallas as pl
from jax.experimental.pallas import tpu as pltpu
from jax.sharding import PartitionSpec as P


def dispatch_rows(send_x, send_rel):
    result = (
        lax.all_to_all(send_x, ("tok", "feat"), split_axis=0, concat_axis=0, tiled=True),
        lax.all_to_all(send_rel, ("tok", "feat"), split_axis=0, concat_axis=0, tiled=True),
    )
    return result


def return_partials(partial_value):
    result = lax.all_to_all(partial_value, ("tok", "feat"), split_axis=0, concat_axis=0, tiled=True)
    return result


def dispatch_errors(send_err):
    result = lax.all_to_all(send_err, ("tok", "feat"), split_axis=0, concat_axis=0, tiled=True)
    return result


def routed_plan(activations, block_lists, top_positions, enc_weight, enc_bias, dec_weight, dec_bias):
    owner_count = lax.axis_size(("tok", "feat"))
    token_count, model_width = activations.shape
    block_rows, active_count = block_lists.shape
    group_rows = token_count // block_rows
    feat_block = enc_weight.shape[1]
    top_count = top_positions.shape[1]
    slot_count = max(2, 3 * token_count * active_count // (2 * group_rows * owner_count))
    per_owner = slot_count * group_rows
    buffer_rows = owner_count * per_owner
    pair_count = block_rows * active_count
    pair_ids = block_lists.reshape(pair_count)
    pair_order = jnp.arange(pair_count, dtype=jnp.int32)
    earlier = (pair_ids[:, None] == pair_ids[None, :]) & (pair_order[None, :] < pair_order[:, None])
    pair_rank = jnp.sum(earlier.astype(jnp.int32), axis=1)
    lane_index = jnp.arange(group_rows, dtype=jnp.int32)
    target = (
        (pair_ids * per_owner + pair_rank * group_rows)[:, None] + lane_index[None, :]
    ).reshape(-1)
    source = ((pair_order // active_count * group_rows)[:, None] + lane_index[None, :]).reshape(-1)
    column = jnp.repeat(pair_order % active_count, group_rows)
    slot_index = jnp.arange(buffer_rows, dtype=jnp.int32)
    hit_bool = slot_index[:, None] == target[None, :]
    hit_float = hit_bool.astype(jnp.float32)
    place_float = jnp.sum(
        hit_float.reshape(buffer_rows, block_rows, active_count, group_rows), axis=2
    ).reshape(buffer_rows, token_count)
    place = place_float.astype(jnp.bfloat16)
    filled = jnp.sum(place_float, axis=1)
    send_x = jnp.dot(place, activations, preferred_element_type=jnp.float32).astype(jnp.bfloat16)
    offsets = top_positions[source] - column[:, None] * feat_block
    offsets = jnp.where((offsets >= 0) & (offsets < feat_block), offsets, feat_block)
    rel_float = (
        jnp.dot(hit_float, offsets.astype(jnp.float32), precision=lax.Precision.HIGHEST)
        + (1.0 - filled)[:, None] * feat_block
    )
    send_rel = rel_float.astype(jnp.int32)
    recv_x, recv_rel = dispatch_rows(
        send_x.reshape(owner_count, per_owner, model_width),
        send_rel.reshape(owner_count, per_owner, top_count),
    )
    recv_x = recv_x.reshape(buffer_rows, model_width)
    recv_rel = recv_rel.reshape(buffer_rows, top_count)
    feature_iota = jnp.arange(feat_block, dtype=jnp.int32)
    mask_bool = jnp.zeros((buffer_rows, feat_block), jnp.bool_)
    for begin in range(0, top_count, 8):
        piece = recv_rel[:, begin : begin + 8]
        mask_bool = mask_bool | jnp.any(piece[:, :, None] == feature_iota[None, None, :], axis=1)
    feat_mask = mask_bool.astype(jnp.float32)
    pre_acts = jnp.dot(recv_x, enc_weight, preferred_element_type=jnp.float32) + enc_bias
    code_vals = (feat_mask * pre_acts).astype(jnp.bfloat16)
    partial_value = jnp.dot(code_vals, dec_weight, preferred_element_type=jnp.float32).astype(
        jnp.bfloat16
    )
    returned = return_partials(partial_value.reshape(owner_count, per_owner, model_width)).reshape(
        buffer_rows, model_width
    )
    summed = lax.dot_general(
        place, returned, (((0,), (0,)), ((), ())), preferred_element_type=jnp.float32
    )
    residual = (summed + dec_bias - activations.astype(jnp.float32)).astype(jnp.bfloat16)
    send_err = jnp.dot(place, residual, preferred_element_type=jnp.float32).astype(jnp.bfloat16)
    recv_err = dispatch_errors(send_err.reshape(owner_count, per_owner, model_width)).reshape(
        buffer_rows, model_width
    )
    grad_codes = lax.dot_general(
        recv_err, dec_weight, (((1,), (1,)), ((), ())), preferred_element_type=jnp.float32
    )
    grad_pre = (feat_mask * grad_codes).astype(jnp.bfloat16)
    enc_grad = lax.dot_general(
        recv_x, grad_pre, (((0,), (0,)), ((), ())), preferred_element_type=jnp.float32
    ).astype(jnp.bfloat16)
    raw_grad = lax.dot_general(
        code_vals, recv_err, (((0,), (0,)), ((), ())), preferred_element_type=jnp.float32
    )
    dec_float = dec_weight.astype(jnp.float32)
    along_coef = jnp.sum(raw_grad * dec_float, axis=1) / (
        jnp.sum(dec_float * dec_float, axis=1) + 1e-06
    )
    dec_grad = (raw_grad - along_coef[:, None] * dec_float).astype(jnp.bfloat16)
    return (enc_grad, dec_grad)


GROUP = ("tok", "feat")


def global_ids(block_lists, top_positions, feat_block):
    token_count = top_positions.shape[0]
    block_rows, active_count = block_lists.shape
    lists = jnp.repeat(block_lists, token_count // block_rows, axis=0)
    column = top_positions // feat_block
    chosen = jnp.zeros_like(top_positions)
    for k in range(active_count):
        chosen = jnp.where(column == k, lists[:, k : k + 1], chosen)
    return chosen * feat_block + top_positions % feat_block


MESH = pl.DeviceIdType.MESH


def place_in_group(zs):
    tok, z = lax.axis_index("tok"), lax.axis_index("feat")
    y, core = tok // 2, tok % 2
    links = {
        "core": {"tok": y * 2 + (1 - core)},
        "y": {"tok": (1 - y) * 2 + core},
        "up": {"feat": jnp.minimum(z + 1, zs - 1)},
        "down": {"feat": jnp.maximum(z - 1, 0)},
    }
    return y, core, z, links


def greet(z, zs, links):
    barrier = pltpu.get_barrier_semaphore()
    for kind in ("core", "y"):
        pl.semaphore_signal(barrier, inc=1, device_id=links[kind], device_id_type=MESH)

    @pl.when(z < zs - 1)
    def _():
        pl.semaphore_signal(barrier, inc=1, device_id=links["up"], device_id_type=MESH)

    @pl.when(z > 0)
    def _():
        pl.semaphore_signal(barrier, inc=1, device_id=links["down"], device_id_type=MESH)

    pl.semaphore_wait(barrier, 2 + jnp.minimum(z, 1) + jnp.minimum(zs - 1 - z, 1))


KINDS = ("up", "down", "y", "core")


def gather_flow(zs, splits, sources, gathered, send, recv, own, consume):
    count = len(splits)
    y, core, z, links = place_in_group(zs)
    pieces = [(a, p) for a in range(count) for p in range(splits[a])]

    def block(yy, cc, zz):
        return (yy * 2 + cc) * zs + zz

    mine = block(y, core, z)

    def rows_of(a, p, b):
        step = sources[a].shape[0] // splits[a]
        return gathered[a].at[pl.ds(b * sources[a].shape[0] + p * step, step)]

    def copy(kind, i, b, from_source=False):
        a, p = pieces[i]
        step = sources[a].shape[0] // splits[a]
        rows = rows_of(a, p, b)
        return pltpu.make_async_remote_copy(
            src_ref=sources[a].at[pl.ds(p * step, step)] if from_source else rows,
            dst_ref=rows,
            send_sem=send.at[KINDS.index(kind), b, i],
            recv_sem=recv.at[b, i],
            device_id=links[kind],
            device_id_type=MESH,
        )

    greet(z, zs, links)
    kept = []
    for a in range(count):
        total = sources[a].shape[0]
        kept.append(
            pltpu.make_async_copy(
                sources[a], gathered[a].at[pl.ds(mine * total, total)], own.at[a]
            )
        )
        kept[-1].start()
    order = list(range(len(pieces)))
    for i in order:

        @pl.when(z < zs - 1)
        def _():
            copy("up", i, mine, True).start()

        @pl.when(z > 0)
        def _():
            copy("down", i, mine, True).start()

        copy("y", i, mine, True).start()
        copy("core", i, mine, True).start()

    def at_distance(d):
        if d == 0:
            return [(None, z, None, None)]
        return [
            (z - d >= 0, z - d, "up", z < zs - 1),
            (z + d < zs, z + d, "down", z > 0),
        ]

    def use(d, yy):
        def pair(zz):
            for i in order:
                copy("core", i, block(yy, 1 - core, zz)).wait_recv()
            consume(block(yy, 0, zz), block(yy, 1, zz))

        def side(k, carry):
            zz = z - d + 2 * d * k
            pl.when((zz >= 0) & (zz < zs))(lambda: pair(zz))
            return carry

        if d == 0:
            pair(z)
        else:
            lax.fori_loop(0, 2, side, 0)

    for d in range(1, zs + 1):
        for i in order:
            if d < zs:
                for valid, zz, kind, onward in at_distance(d):

                    @pl.when(valid)
                    def _():
                        b = block(y, core, zz)
                        copy("core", i, b).wait_recv()

                        @pl.when(onward)
                        def _():
                            copy(kind, i, b).start()

                        copy("y", i, b).start()
                        copy("core", i, b).start()

            for valid, zz, kind, onward in at_distance(d - 1):

                def pass_on():
                    b = block(1 - y, core, zz)
                    copy("core", i, b).wait_recv()
                    copy("core", i, b).start()

                if valid is None:
                    pass_on()
                else:
                    pl.when(valid)(pass_on)
        if d == 1:
            for a in range(count):
                kept[a].wait()
        use(d - 1, y)
        if d > 1:
            use(d - 2, 1 - y)
    use(zs - 1, 1 - y)
    for i in order:

        @pl.when(z < zs - 1)
        def _():
            copy("up", i, mine, True).wait_send()

        @pl.when(z > 0)
        def _():
            copy("down", i, mine, True).wait_send()

        copy("y", i, mine, True).wait_send()
        copy("core", i, mine, True).wait_send()
        for d in range(1, zs):
            for valid, zz, kind, onward in at_distance(d):

                @pl.when(valid)
                def _():
                    b = block(y, core, zz)

                    @pl.when(onward)
                    def _():
                        copy(kind, i, b).wait_send()

                    copy("y", i, b).wait_send()
                    copy("core", i, b).wait_send()

        for zz in range(zs):
            copy("core", i, block(1 - y, core, zz)).wait_send()


def pair_rows(first, second, rows):
    return [pl.ds(pl.multiple_of(b * rows, rows), rows) for b in (first, second)]


def encode_kernel(
    zs, splits, x_ref, ids_ref, enc_ref, bias_ref, all_x, codes_ref, mask_ref,
    all_ids, buf, hits, send, recv, own, load,
):
    rows, feat_block = x_ref.shape[0], enc_ref.shape[1]
    base = (lax.axis_index("tok") * zs + lax.axis_index("feat")) * feat_block
    strip = 32

    def consume(first, second):
        spans = pair_rows(first, second, rows)
        loads = [
            pltpu.make_async_copy(all_x.at[span], buf.at[pl.ds(k * rows, rows)], load.at[k])
            for k, span in enumerate(spans)
        ]
        for one in loads:
            one.start()
        for k, b in enumerate((first, second)):

            def mark(j, carry):
                begin = pl.multiple_of(b * rows + j * strip, strip)
                rel = all_ids[pl.ds(begin, strip), :] - base
                feature = lax.broadcasted_iota(jnp.int32, (strip, feat_block), 1)
                found = jnp.zeros((strip, feat_block), jnp.float32)
                for t in range(rel.shape[1]):
                    found = jnp.where(rel[:, t : t + 1] == feature, 1.0, found)
                hits[pl.ds(pl.multiple_of(k * rows + j * strip, strip), strip), :] = found
                return carry

            lax.fori_loop(0, rows // strip, mark, 0)
        for one in loads:
            one.wait()
        pre = jnp.dot(buf[...], enc_ref[...], preferred_element_type=jnp.float32) + bias_ref[...]
        found = hits[...]
        codes = jnp.where(found > 0, pre, 0.0).astype(jnp.bfloat16)
        for k, span in enumerate(spans):
            codes_ref[span, :] = codes[k * rows : (k + 1) * rows]
            mask_ref[span, :] = found[k * rows : (k + 1) * rows].astype(jnp.bfloat16)

    gather_flow(zs, splits, (ids_ref, x_ref), (all_ids, all_x), send, recv, own, consume)


def gather_sems(owner_count, pieces, arrays):
    return [
        pltpu.SemaphoreType.DMA((len(KINDS), owner_count, pieces)),
        pltpu.SemaphoreType.DMA((owner_count, pieces)),
        pltpu.SemaphoreType.DMA((arrays,)),
        pltpu.SemaphoreType.DMA((2,)),
    ]


def encode_rows(x, ids, enc_weight, enc_bias, collective_id):
    owner_count, zs = lax.axis_size(GROUP), lax.axis_size("feat")
    rows, width = x.shape
    feat_block = enc_weight.shape[1]
    total = owner_count * rows
    splits = (1, 2)
    vmem, hbm = pl.BlockSpec(memory_space=pltpu.VMEM), pl.BlockSpec(memory_space=pl.ANY)
    return pl.pallas_call(
        functools.partial(encode_kernel, zs, splits),
        out_shape=[
            jax.ShapeDtypeStruct((total, width), x.dtype),
            jax.ShapeDtypeStruct((total, feat_block), jnp.bfloat16),
            jax.ShapeDtypeStruct((total, feat_block), jnp.bfloat16),
        ],
        in_specs=[hbm, hbm, vmem, vmem],
        out_specs=[hbm, vmem, vmem],
        scratch_shapes=[
            pltpu.VMEM((total, ids.shape[1]), jnp.int32),
            pltpu.VMEM((2 * rows, width), jnp.bfloat16),
            pltpu.VMEM((2 * rows, feat_block), jnp.float32),
        ]
        + gather_sems(owner_count, sum(splits), 2),
        compiler_params=pltpu.CompilerParams(
            collective_id=collective_id, has_side_effects=True, vmem_limit_bytes=32 * 1024 * 1024
        ),
        name="encode_rows",
    )(x, ids, enc_weight, enc_bias.reshape(1, feat_block))


def grads_kernel(
    zs, splits, err_ref, all_x, codes_ref, mask_ref, dec_ref, enc_out, dec_out,
    all_err, buf, enc_acc, raw_acc, send, recv, own, load,
):
    rows, width = err_ref.shape
    feat_block = dec_ref.shape[0]
    tile, strip = 768, 16

    def clear(j, carry):
        span = pl.ds(pl.multiple_of(j * strip, strip), strip)
        enc_acc[span, :] = jnp.zeros((strip, width), jnp.float32)
        raw_acc[span, :] = jnp.zeros((strip, width), jnp.float32)
        return carry

    def pair_of(ref, spans, cols=slice(None)):
        return jnp.concatenate([ref[span, cols] for span in spans], axis=0)

    def consume(first, second):
        spans = pair_rows(first, second, rows)
        loads = [
            pltpu.make_async_copy(all_x.at[span], buf.at[pl.ds(k * rows, rows)], load.at[k])
            for k, span in enumerate(spans)
        ]
        for one in loads:
            one.start()
        grads = lax.dot_general(
            pair_of(all_err, spans), dec_ref[...], (((1,), (1,)), ((), ())),
            preferred_element_type=jnp.float32,
        )
        grads = jnp.where(pair_of(mask_ref, spans) > 0, grads, 0.0).astype(jnp.bfloat16)
        codes = pair_of(codes_ref, spans)
        for one in loads:
            one.wait()

        def add(j, carry):
            cols = pl.ds(pl.multiple_of(j * tile, tile), tile)
            raw_acc[:, cols] += lax.dot_general(
                codes, pair_of(all_err, spans, cols), (((0,), (0,)), ((), ())),
                preferred_element_type=jnp.float32,
            )
            enc_acc[:, cols] += lax.dot_general(
                grads, buf[:, cols], (((0,), (0,)), ((), ())),
                preferred_element_type=jnp.float32,
            )
            return carry

        lax.fori_loop(0, width // tile, add, 0)

    lax.fori_loop(0, feat_block // strip, clear, 0)
    gather_flow(zs, splits, (err_ref,), (all_err,), send, recv, own, consume)

    def finish(j, carry):
        span = pl.ds(pl.multiple_of(j * strip, strip), strip)
        raw = raw_acc[span, :]
        dec = dec_ref[span, :].astype(jnp.float32)
        coef = jnp.sum(raw * dec, axis=1, keepdims=True) / (
            jnp.sum(dec * dec, axis=1, keepdims=True) + 1e-06
        )
        dec_out[span, :] = (raw - coef * dec).astype(jnp.bfloat16)
        enc_out[span, :] = enc_acc[span, :].astype(jnp.bfloat16)
        return carry

    lax.fori_loop(0, feat_block // strip, finish, 0)


def gradient_rows(residual, all_x, codes, mask, dec_weight, collective_id):
    owner_count, zs = lax.axis_size(GROUP), lax.axis_size("feat")
    rows, width = residual.shape
    feat_block = dec_weight.shape[0]
    splits = (2,)
    vmem, hbm = pl.BlockSpec(memory_space=pltpu.VMEM), pl.BlockSpec(memory_space=pl.ANY)
    return pl.pallas_call(
        functools.partial(grads_kernel, zs, splits),
        out_shape=[jax.ShapeDtypeStruct((feat_block, width), jnp.bfloat16)] * 2,
        in_specs=[hbm, hbm, vmem, vmem, vmem],
        out_specs=[vmem, vmem],
        scratch_shapes=[
            pltpu.VMEM((owner_count * rows, width), jnp.bfloat16),
            pltpu.VMEM((2 * rows, width), jnp.bfloat16),
            pltpu.VMEM((feat_block, width), jnp.float32),
            pltpu.VMEM((feat_block, width), jnp.float32),
        ]
        + gather_sems(owner_count, sum(splits), 1),
        compiler_params=pltpu.CompilerParams(
            collective_id=collective_id, has_side_effects=True, vmem_limit_bytes=56 * 1024 * 1024
        ),
        name="gradient_rows",
    )(residual, all_x, codes, mask, dec_weight)


def reduce_kernel(
    zs, x_ref, bias_ref, codes_ref, dec_ref, out_ref,
    a_out, a_in, b_out, b_in, c_out, c_in, a_send, a_recv, b_send, b_recv, c_send, c_recv,
):
    y, core, z, links = place_in_group(zs)
    rows, width = out_ref.shape
    tile = 768

    def product(yy, cc, zz, added, write):
        begin = pl.multiple_of(((yy * 2 + cc) * zs + zz) * rows, rows)

        def body(j, carry):
            cols = pl.ds(pl.multiple_of(j * tile, tile), tile)
            acc = jnp.dot(
                codes_ref[pl.ds(begin, rows), :], dec_ref[:, cols],
                preferred_element_type=jnp.float32,
            )
            for read in added:
                acc += read(cols).astype(jnp.float32)
            write(cols, acc)
            return carry

        lax.fori_loop(0, width // tile, body, 0)

    def store_at(ref, slot):
        def write(cols, acc):
            ref[slot, :, cols] = acc.astype(jnp.bfloat16)

        return write

    def load_at(ref, *slot):
        return lambda cols: ref[(*slot, slice(None), cols)]

    def copy_a(slot):
        return pltpu.make_async_remote_copy(
            src_ref=a_out.at[slot], dst_ref=a_in.at[slot], send_sem=a_send.at[slot],
            recv_sem=a_recv.at[slot], device_id=links["core"], device_id_type=MESH,
        )

    def copy_b(zz):
        return pltpu.make_async_remote_copy(
            src_ref=b_out.at[zz], dst_ref=b_in.at[zz], send_sem=b_send.at[zz],
            recv_sem=b_recv.at[zz], device_id=links["y"], device_id_type=MESH,
        )

    def copy_c(way, zz):
        return pltpu.make_async_remote_copy(
            src_ref=c_out.at[zz], dst_ref=c_in.at[way, zz], send_sem=c_send.at[zz],
            recv_sem=c_recv.at[way, zz], device_id=links["up" if way == 0 else "down"],
            device_id_type=MESH,
        )

    rounds = []
    for d in range(zs - 1, 0, -1):
        rounds.append((z + d < zs, z + d, 0))
        rounds.append((z - d >= 0, z - d, 1))
    rounds.append((None, z, None))

    def run(valid, action):
        if valid is None:
            action()
        else:
            pl.when(valid)(action)

    greet(z, zs, links)
    for valid, zz, way in rounds:

        def pair_step():
            for yy in (1 - y, y):
                slot = yy * zs + zz
                product(yy, 1 - core, zz, (), store_at(a_out, slot))
                copy_a(slot).start()
            slot = (1 - y) * zs + zz
            copy_a(slot).wait_recv()
            product(1 - y, core, zz, (load_at(a_in, slot),), store_at(b_out, zz))
            copy_b(zz).start()

        run(valid, pair_step)
    for valid, zz, way in rounds[:-1]:
        first = (z == 0) if way == 0 else (z == zs - 1)

        def line_step():
            slot = y * zs + zz
            copy_a(slot).wait_recv()
            copy_b(zz).wait_recv()
            near = (load_at(a_in, slot), load_at(b_in, zz))

            @pl.when(first)
            def _():
                product(y, core, zz, near, store_at(c_out, zz))

            @pl.when(jnp.logical_not(first))
            def _():
                copy_c(way, zz).wait_recv()
                product(y, core, zz, near + (load_at(c_in, way, zz),), store_at(c_out, zz))

            copy_c(way, zz).start()

        run(valid, line_step)
    slot = y * zs + z
    copy_a(slot).wait_recv()
    copy_b(z).wait_recv()

    def finish(cols, acc):
        out_ref[:, cols] = (
            acc + bias_ref[:, cols] - x_ref[:, cols].astype(jnp.float32)
        ).astype(jnp.bfloat16)

    near = (load_at(a_in, slot), load_at(b_in, z))

    @pl.when(z == 0)
    def _():
        copy_c(1, z).wait_recv()
        product(y, core, z, near + (load_at(c_in, 1, z),), finish)

    @pl.when(z == zs - 1)
    def _():
        copy_c(0, z).wait_recv()
        product(y, core, z, near + (load_at(c_in, 0, z),), finish)

    @pl.when((z > 0) & (z < zs - 1))
    def _():
        copy_c(1, z).wait_recv()
        copy_c(0, z).wait_recv()
        product(y, core, z, near + (load_at(c_in, 0, z), load_at(c_in, 1, z)), finish)

    for slot in range(2 * zs):
        copy_a(slot).wait_send()
    for zz in range(zs):
        copy_b(zz).wait_send()
    for valid, zz, way in rounds[:-1]:
        run(valid, lambda: copy_c(way, zz).wait_send())


def reduce_rows(x, bias, codes, dec_weight, collective_id):
    zs = lax.axis_size("feat")
    rows, width = x.shape
    slab = lambda *lead: pltpu.VMEM(lead + (rows, width), jnp.bfloat16)
    sem = lambda *lead: pltpu.SemaphoreType.DMA(lead)
    return pl.pallas_call(
        functools.partial(reduce_kernel, zs),
        out_shape=jax.ShapeDtypeStruct((rows, width), jnp.bfloat16),
        in_specs=[pl.BlockSpec(memory_space=pltpu.VMEM)] * 4,
        out_specs=pl.BlockSpec(memory_space=pltpu.VMEM),
        scratch_shapes=[
            slab(2 * zs), slab(2 * zs), slab(zs), slab(zs), slab(zs), slab(2, zs),
            sem(2 * zs), sem(2 * zs), sem(zs), sem(zs), sem(zs), sem(2, zs),
        ],
        compiler_params=pltpu.CompilerParams(
            collective_id=collective_id, has_side_effects=True, vmem_limit_bytes=48 * 1024 * 1024
        ),
        name="reduce_rows",
    )(x, bias.reshape(1, width), codes, dec_weight)


def gathered_plan(activations, block_lists, top_positions, enc_weight, enc_bias, dec_weight, dec_bias):
    ids = global_ids(block_lists, top_positions, enc_weight.shape[1])
    all_x, code_vals, mask = encode_rows(activations, ids, enc_weight, enc_bias, 1)
    residual = reduce_rows(activations, dec_bias, code_vals, dec_weight, 2)
    enc_turned, dec_grad = gradient_rows(residual, all_x, code_vals, mask, dec_weight, 3)
    return (enc_turned.T, dec_grad)


def on_device(activations, block_lists, top_positions, *weights):
    owner_count = lax.axis_size(GROUP)
    pairs = activations.shape[0] * block_lists.shape[1]
    gathered = owner_count * activations.shape[0]
    square = lax.axis_size("tok") == 4 and activations.shape[1] % 768 == 0
    if square and gathered <= 4 * pairs:
        return gathered_plan(activations, block_lists, top_positions, *weights)
    return routed_plan(activations, block_lists, top_positions, *weights)


def solution(mesh):
    placed = (
        P(("grp", "tok", "feat"), None),
        P(("grp", "tok", "feat"), None),
        P(("grp", "tok", "feat"), None),
        P(None, ("tok", "feat")),
        P(("tok", "feat")),
        P(("tok", "feat"), None),
        P(),
    )
    return jax.shard_map(
        on_device,
        mesh=mesh,
        in_specs=placed,
        out_specs=(P(None, ("grp", "tok", "feat")), P(("grp", "tok", "feat"), None)),
        check_vma=False,
    )
```

```python
import functools

import jax
import jax.numpy as jnp
from jax import lax
from jax.experimental import pallas as pl
from jax.experimental.pallas import tpu as pltpu
from jax.sharding import PartitionSpec as P


def dispatch_rows(send_x, send_rel):
    result = (
        lax.all_to_all(send_x, ("tok", "feat"), split_axis=0, concat_axis=0, tiled=True),
        lax.all_to_all(send_rel, ("tok", "feat"), split_axis=0, concat_axis=0, tiled=True),
    )
    return result


def return_partials(partial_value):
    result = lax.all_to_all(partial_value, ("tok", "feat"), split_axis=0, concat_axis=0, tiled=True)
    return result


def dispatch_errors(send_err):
    result = lax.all_to_all(send_err, ("tok", "feat"), split_axis=0, concat_axis=0, tiled=True)
    return result


def routed_plan(activations, block_lists, top_positions, enc_weight, enc_bias, dec_weight, dec_bias):
    owner_count = lax.axis_size(("tok", "feat"))
    token_count, model_width = activations.shape
    block_rows, active_count = block_lists.shape
    group_rows = token_count // block_rows
    feat_block = enc_weight.shape[1]
    top_count = top_positions.shape[1]
    slot_count = max(2, 3 * token_count * active_count // (2 * group_rows * owner_count))
    per_owner = slot_count * group_rows
    buffer_rows = owner_count * per_owner
    pair_count = block_rows * active_count
    pair_ids = block_lists.reshape(pair_count)
    pair_order = jnp.arange(pair_count, dtype=jnp.int32)
    earlier = (pair_ids[:, None] == pair_ids[None, :]) & (pair_order[None, :] < pair_order[:, None])
    pair_rank = jnp.sum(earlier.astype(jnp.int32), axis=1)
    lane_index = jnp.arange(group_rows, dtype=jnp.int32)
    target = (
        (pair_ids * per_owner + pair_rank * group_rows)[:, None] + lane_index[None, :]
    ).reshape(-1)
    source = ((pair_order // active_count * group_rows)[:, None] + lane_index[None, :]).reshape(-1)
    column = jnp.repeat(pair_order % active_count, group_rows)
    slot_index = jnp.arange(buffer_rows, dtype=jnp.int32)
    hit_bool = slot_index[:, None] == target[None, :]
    hit_float = hit_bool.astype(jnp.float32)
    place_float = jnp.sum(
        hit_float.reshape(buffer_rows, block_rows, active_count, group_rows), axis=2
    ).reshape(buffer_rows, token_count)
    place = place_float.astype(jnp.bfloat16)
    filled = jnp.sum(place_float, axis=1)
    send_x = jnp.dot(place, activations, preferred_element_type=jnp.float32).astype(jnp.bfloat16)
    offsets = top_positions[source] - column[:, None] * feat_block
    offsets = jnp.where((offsets >= 0) & (offsets < feat_block), offsets, feat_block)
    rel_float = (
        jnp.dot(hit_float, offsets.astype(jnp.float32), precision=lax.Precision.HIGHEST)
        + (1.0 - filled)[:, None] * feat_block
    )
    send_rel = rel_float.astype(jnp.int32)
    recv_x, recv_rel = dispatch_rows(
        send_x.reshape(owner_count, per_owner, model_width),
        send_rel.reshape(owner_count, per_owner, top_count),
    )
    recv_x = recv_x.reshape(buffer_rows, model_width)
    recv_rel = recv_rel.reshape(buffer_rows, top_count)
    feature_iota = jnp.arange(feat_block, dtype=jnp.int32)
    mask_bool = jnp.zeros((buffer_rows, feat_block), jnp.bool_)
    for begin in range(0, top_count, 8):
        piece = recv_rel[:, begin : begin + 8]
        mask_bool = mask_bool | jnp.any(piece[:, :, None] == feature_iota[None, None, :], axis=1)
    feat_mask = mask_bool.astype(jnp.float32)
    pre_acts = jnp.dot(recv_x, enc_weight, preferred_element_type=jnp.float32) + enc_bias
    code_vals = (feat_mask * pre_acts).astype(jnp.bfloat16)
    partial_value = jnp.dot(code_vals, dec_weight, preferred_element_type=jnp.float32).astype(
        jnp.bfloat16
    )
    returned = return_partials(partial_value.reshape(owner_count, per_owner, model_width)).reshape(
        buffer_rows, model_width
    )
    summed = lax.dot_general(
        place, returned, (((0,), (0,)), ((), ())), preferred_element_type=jnp.float32
    )
    residual = (summed + dec_bias - activations.astype(jnp.float32)).astype(jnp.bfloat16)
    send_err = jnp.dot(place, residual, preferred_element_type=jnp.float32).astype(jnp.bfloat16)
    recv_err = dispatch_errors(send_err.reshape(owner_count, per_owner, model_width)).reshape(
        buffer_rows, model_width
    )
    grad_codes = lax.dot_general(
        recv_err, dec_weight, (((1,), (1,)), ((), ())), preferred_element_type=jnp.float32
    )
    grad_pre = (feat_mask * grad_codes).astype(jnp.bfloat16)
    enc_grad = lax.dot_general(
        recv_x, grad_pre, (((0,), (0,)), ((), ())), preferred_element_type=jnp.float32
    ).astype(jnp.bfloat16)
    raw_grad = lax.dot_general(
        code_vals, recv_err, (((0,), (0,)), ((), ())), preferred_element_type=jnp.float32
    )
    dec_float = dec_weight.astype(jnp.float32)
    along_coef = jnp.sum(raw_grad * dec_float, axis=1) / (
        jnp.sum(dec_float * dec_float, axis=1) + 1e-06
    )
    dec_grad = (raw_grad - along_coef[:, None] * dec_float).astype(jnp.bfloat16)
    return (enc_grad, dec_grad)


GROUP = ("tok", "feat")


def global_ids(block_lists, top_positions, feat_block):
    token_count = top_positions.shape[0]
    block_rows, active_count = block_lists.shape
    lists = jnp.repeat(block_lists, token_count // block_rows, axis=0)
    column = top_positions // feat_block
    chosen = jnp.zeros_like(top_positions)
    for k in range(active_count):
        chosen = jnp.where(column == k, lists[:, k : k + 1], chosen)
    return chosen * feat_block + top_positions % feat_block


MESH = pl.DeviceIdType.MESH


def place_in_group(zs):
    tok, z = lax.axis_index("tok"), lax.axis_index("feat")
    y, core = tok // 2, tok % 2
    links = {
        "core": {"tok": y * 2 + (1 - core)},
        "y": {"tok": (1 - y) * 2 + core},
        "up": {"feat": jnp.minimum(z + 1, zs - 1)},
        "down": {"feat": jnp.maximum(z - 1, 0)},
    }
    return y, core, z, links


def greet(z, zs, links):
    barrier = pltpu.get_barrier_semaphore()
    for kind in ("core", "y"):
        pl.semaphore_signal(barrier, inc=1, device_id=links[kind], device_id_type=MESH)

    @pl.when(z < zs - 1)
    def _():
        pl.semaphore_signal(barrier, inc=1, device_id=links["up"], device_id_type=MESH)

    @pl.when(z > 0)
    def _():
        pl.semaphore_signal(barrier, inc=1, device_id=links["down"], device_id_type=MESH)

    pl.semaphore_wait(barrier, 2 + jnp.minimum(z, 1) + jnp.minimum(zs - 1 - z, 1))


KINDS = ("up", "down", "y", "core")


def gather_flow(zs, splits, sources, gathered, send, recv, own, consume):
    count = len(splits)
    y, core, z, links = place_in_group(zs)
    pieces = [(a, p) for a in range(count) for p in range(splits[a])]

    def block(yy, cc, zz):
        return (yy * 2 + cc) * zs + zz

    mine = block(y, core, z)

    def rows_of(a, p, b):
        step = sources[a].shape[0] // splits[a]
        return gathered[a].at[pl.ds(b * sources[a].shape[0] + p * step, step)]

    def copy(kind, i, b, from_source=False):
        a, p = pieces[i]
        step = sources[a].shape[0] // splits[a]
        rows = rows_of(a, p, b)
        return pltpu.make_async_remote_copy(
            src_ref=sources[a].at[pl.ds(p * step, step)] if from_source else rows,
            dst_ref=rows,
            send_sem=send.at[KINDS.index(kind), b, i],
            recv_sem=recv.at[b, i],
            device_id=links[kind],
            device_id_type=MESH,
        )

    greet(z, zs, links)
    kept = []
    for a in range(count):
        total = sources[a].shape[0]
        kept.append(
            pltpu.make_async_copy(
                sources[a], gathered[a].at[pl.ds(mine * total, total)], own.at[a]
            )
        )
        kept[-1].start()
    order = list(range(len(pieces)))
    for i in order:

        @pl.when(z < zs - 1)
        def _():
            copy("up", i, mine, True).start()

        @pl.when(z > 0)
        def _():
            copy("down", i, mine, True).start()

        copy("y", i, mine, True).start()
        copy("core", i, mine, True).start()

    def at_distance(d):
        if d == 0:
            return [(None, z, None, None)]
        return [
            (z - d >= 0, z - d, "up", z < zs - 1),
            (z + d < zs, z + d, "down", z > 0),
        ]

    def use(d, yy):
        def pair(zz):
            for i in order:
                copy("core", i, block(yy, 1 - core, zz)).wait_recv()
            consume(block(yy, 0, zz), block(yy, 1, zz))

        def side(k, carry):
            zz = z - d + 2 * d * k
            pl.when((zz >= 0) & (zz < zs))(lambda: pair(zz))
            return carry

        if d == 0:
            pair(z)
        else:
            lax.fori_loop(0, 2, side, 0)

    def along_column(d):
        for i in order:
            for valid, zz, kind, onward in at_distance(d):

                @pl.when(valid)
                def _():
                    b = block(y, core, zz)
                    copy("core", i, b).wait_recv()

                    @pl.when(onward)
                    def _():
                        copy(kind, i, b).start()

                    copy("y", i, b).start()
                    copy("core", i, b).start()

    def across(d):
        for i in order:
            for valid, zz, kind, onward in at_distance(d):

                def pass_on():
                    b = block(1 - y, core, zz)
                    copy("core", i, b).wait_recv()
                    copy("core", i, b).start()

                if valid is None:
                    pass_on()
                else:
                    pl.when(valid)(pass_on)

    for d in range(1, zs):
        along_column(d)
        if d == 1:
            for a in range(count):
                kept[a].wait()
        use(d - 1, y)
        if d > 1:
            use(d - 2, 1 - y)
        across(d - 1)
    use(zs - 1, y)
    across(zs - 1)
    use(zs - 2, 1 - y)
    use(zs - 1, 1 - y)
    for i in order:

        @pl.when(z < zs - 1)
        def _():
            copy("up", i, mine, True).wait_send()

        @pl.when(z > 0)
        def _():
            copy("down", i, mine, True).wait_send()

        copy("y", i, mine, True).wait_send()
        copy("core", i, mine, True).wait_send()
        for d in range(1, zs):
            for valid, zz, kind, onward in at_distance(d):

                @pl.when(valid)
                def _():
                    b = block(y, core, zz)

                    @pl.when(onward)
                    def _():
                        copy(kind, i, b).wait_send()

                    copy("y", i, b).wait_send()
                    copy("core", i, b).wait_send()

        for zz in range(zs):
            copy("core", i, block(1 - y, core, zz)).wait_send()


def pair_rows(first, second, rows):
    return [pl.ds(pl.multiple_of(b * rows, rows), rows) for b in (first, second)]


def encode_kernel(
    zs, splits, x_ref, ids_ref, enc_ref, bias_ref, all_x, codes_ref, mask_ref,
    all_ids, buf, hits, send, recv, own, load,
):
    rows, feat_block = x_ref.shape[0], enc_ref.shape[1]
    base = (lax.axis_index("tok") * zs + lax.axis_index("feat")) * feat_block
    strip = 32

    def consume(first, second):
        spans = pair_rows(first, second, rows)
        loads = [
            pltpu.make_async_copy(all_x.at[span], buf.at[pl.ds(k * rows, rows)], load.at[k])
            for k, span in enumerate(spans)
        ]
        for one in loads:
            one.start()
        for k, b in enumerate((first, second)):

            def mark(j, carry):
                begin = pl.multiple_of(b * rows + j * strip, strip)
                rel = all_ids[pl.ds(begin, strip), :] - base
                feature = lax.broadcasted_iota(jnp.int32, (strip, feat_block), 1)
                found = jnp.zeros((strip, feat_block), jnp.float32)
                for t in range(rel.shape[1]):
                    found = jnp.where(rel[:, t : t + 1] == feature, 1.0, found)
                hits[pl.ds(pl.multiple_of(k * rows + j * strip, strip), strip), :] = found
                return carry

            lax.fori_loop(0, rows // strip, mark, 0)
        for one in loads:
            one.wait()
        pre = jnp.dot(buf[...], enc_ref[...], preferred_element_type=jnp.float32) + bias_ref[...]
        found = hits[...]
        codes = jnp.where(found > 0, pre, 0.0).astype(jnp.bfloat16)
        for k, span in enumerate(spans):
            codes_ref[span, :] = codes[k * rows : (k + 1) * rows]
            mask_ref[span, :] = found[k * rows : (k + 1) * rows].astype(jnp.bfloat16)

    gather_flow(zs, splits, (ids_ref, x_ref), (all_ids, all_x), send, recv, own, consume)


def gather_sems(owner_count, pieces, arrays):
    return [
        pltpu.SemaphoreType.DMA((len(KINDS), owner_count, pieces)),
        pltpu.SemaphoreType.DMA((owner_count, pieces)),
        pltpu.SemaphoreType.DMA((arrays,)),
        pltpu.SemaphoreType.DMA((2,)),
    ]


def encode_rows(x, ids, enc_weight, enc_bias, collective_id):
    owner_count, zs = lax.axis_size(GROUP), lax.axis_size("feat")
    rows, width = x.shape
    feat_block = enc_weight.shape[1]
    total = owner_count * rows
    splits = (1, 2)
    vmem, hbm = pl.BlockSpec(memory_space=pltpu.VMEM), pl.BlockSpec(memory_space=pl.ANY)
    return pl.pallas_call(
        functools.partial(encode_kernel, zs, splits),
        out_shape=[
            jax.ShapeDtypeStruct((total, width), x.dtype),
            jax.ShapeDtypeStruct((total, feat_block), jnp.bfloat16),
            jax.ShapeDtypeStruct((total, feat_block), jnp.bfloat16),
        ],
        in_specs=[hbm, hbm, vmem, vmem],
        out_specs=[hbm, vmem, vmem],
        scratch_shapes=[
            pltpu.VMEM((total, ids.shape[1]), jnp.int32),
            pltpu.VMEM((2 * rows, width), jnp.bfloat16),
            pltpu.VMEM((2 * rows, feat_block), jnp.float32),
        ]
        + gather_sems(owner_count, sum(splits), 2),
        compiler_params=pltpu.CompilerParams(
            collective_id=collective_id, has_side_effects=True, vmem_limit_bytes=32 * 1024 * 1024
        ),
        name="encode_rows",
    )(x, ids, enc_weight, enc_bias.reshape(1, feat_block))


def grads_kernel(
    zs, splits, err_ref, all_x, codes_ref, mask_ref, dec_ref, enc_out, dec_out,
    all_err, buf, enc_acc, raw_acc, send, recv, own, load,
):
    rows, width = err_ref.shape
    feat_block = dec_ref.shape[0]
    tile, strip = 768, 16

    def clear(j, carry):
        span = pl.ds(pl.multiple_of(j * strip, strip), strip)
        enc_acc[span, :] = jnp.zeros((strip, width), jnp.float32)
        raw_acc[span, :] = jnp.zeros((strip, width), jnp.float32)
        return carry

    def pair_of(ref, spans, cols=slice(None)):
        return jnp.concatenate([ref[span, cols] for span in spans], axis=0)

    def consume(first, second):
        spans = pair_rows(first, second, rows)
        loads = [
            pltpu.make_async_copy(all_x.at[span], buf.at[pl.ds(k * rows, rows)], load.at[k])
            for k, span in enumerate(spans)
        ]
        for one in loads:
            one.start()
        grads = lax.dot_general(
            pair_of(all_err, spans), dec_ref[...], (((1,), (1,)), ((), ())),
            preferred_element_type=jnp.float32,
        )
        grads = jnp.where(pair_of(mask_ref, spans) > 0, grads, 0.0).astype(jnp.bfloat16)
        codes = pair_of(codes_ref, spans)
        for one in loads:
            one.wait()

        def add(j, carry):
            cols = pl.ds(pl.multiple_of(j * tile, tile), tile)
            raw_acc[:, cols] += lax.dot_general(
                codes, pair_of(all_err, spans, cols), (((0,), (0,)), ((), ())),
                preferred_element_type=jnp.float32,
            )
            enc_acc[:, cols] += lax.dot_general(
                grads, buf[:, cols], (((0,), (0,)), ((), ())),
                preferred_element_type=jnp.float32,
            )
            return carry

        lax.fori_loop(0, width // tile, add, 0)

    lax.fori_loop(0, feat_block // strip, clear, 0)
    gather_flow(zs, splits, (err_ref,), (all_err,), send, recv, own, consume)

    def finish(j, carry):
        span = pl.ds(pl.multiple_of(j * strip, strip), strip)
        raw = raw_acc[span, :]
        dec = dec_ref[span, :].astype(jnp.float32)
        coef = jnp.sum(raw * dec, axis=1, keepdims=True) / (
            jnp.sum(dec * dec, axis=1, keepdims=True) + 1e-06
        )
        dec_out[span, :] = (raw - coef * dec).astype(jnp.bfloat16)
        enc_out[span, :] = enc_acc[span, :].astype(jnp.bfloat16)
        return carry

    lax.fori_loop(0, feat_block // strip, finish, 0)


def gradient_rows(residual, all_x, codes, mask, dec_weight, collective_id):
    owner_count, zs = lax.axis_size(GROUP), lax.axis_size("feat")
    rows, width = residual.shape
    feat_block = dec_weight.shape[0]
    splits = (2,)
    vmem, hbm = pl.BlockSpec(memory_space=pltpu.VMEM), pl.BlockSpec(memory_space=pl.ANY)
    return pl.pallas_call(
        functools.partial(grads_kernel, zs, splits),
        out_shape=[jax.ShapeDtypeStruct((feat_block, width), jnp.bfloat16)] * 2,
        in_specs=[hbm, hbm, vmem, vmem, vmem],
        out_specs=[vmem, vmem],
        scratch_shapes=[
            pltpu.VMEM((owner_count * rows, width), jnp.bfloat16),
            pltpu.VMEM((2 * rows, width), jnp.bfloat16),
            pltpu.VMEM((feat_block, width), jnp.float32),
            pltpu.VMEM((feat_block, width), jnp.float32),
        ]
        + gather_sems(owner_count, sum(splits), 1),
        compiler_params=pltpu.CompilerParams(
            collective_id=collective_id, has_side_effects=True, vmem_limit_bytes=56 * 1024 * 1024
        ),
        name="gradient_rows",
    )(residual, all_x, codes, mask, dec_weight)


def reduce_kernel(
    zs, x_ref, bias_ref, codes_ref, dec_ref, out_ref,
    a_out, a_in, b_out, b_in, c_out, c_in, a_send, a_recv, b_send, b_recv, c_send, c_recv,
):
    y, core, z, links = place_in_group(zs)
    rows, width = out_ref.shape
    tile = 768

    def product(yy, cc, zz, added, write):
        begin = pl.multiple_of(((yy * 2 + cc) * zs + zz) * rows, rows)

        def body(j, carry):
            cols = pl.ds(pl.multiple_of(j * tile, tile), tile)
            acc = jnp.dot(
                codes_ref[pl.ds(begin, rows), :], dec_ref[:, cols],
                preferred_element_type=jnp.float32,
            )
            for read in added:
                acc += read(cols).astype(jnp.float32)
            write(cols, acc)
            return carry

        lax.fori_loop(0, width // tile, body, 0)

    def store_at(ref, slot):
        def write(cols, acc):
            ref[slot, :, cols] = acc.astype(jnp.bfloat16)

        return write

    def load_at(ref, *slot):
        return lambda cols: ref[(*slot, slice(None), cols)]

    def copy_a(slot):
        return pltpu.make_async_remote_copy(
            src_ref=a_out.at[slot], dst_ref=a_in.at[slot], send_sem=a_send.at[slot],
            recv_sem=a_recv.at[slot], device_id=links["core"], device_id_type=MESH,
        )

    def copy_b(zz):
        return pltpu.make_async_remote_copy(
            src_ref=b_out.at[zz], dst_ref=b_in.at[zz], send_sem=b_send.at[zz],
            recv_sem=b_recv.at[zz], device_id=links["y"], device_id_type=MESH,
        )

    def copy_c(way, zz):
        return pltpu.make_async_remote_copy(
            src_ref=c_out.at[zz], dst_ref=c_in.at[way, zz], send_sem=c_send.at[zz],
            recv_sem=c_recv.at[way, zz], device_id=links["up" if way == 0 else "down"],
            device_id_type=MESH,
        )

    rounds = []
    for d in range(zs - 1, 0, -1):
        rounds.append((z + d < zs, z + d, 0))
        rounds.append((z - d >= 0, z - d, 1))
    rounds.append((None, z, None))

    def run(valid, action):
        if valid is None:
            action()
        else:
            pl.when(valid)(action)

    greet(z, zs, links)
    for valid, zz, way in rounds:

        def pair_step():
            for yy in (1 - y, y):
                slot = yy * zs + zz
                product(yy, 1 - core, zz, (), store_at(a_out, slot))
                copy_a(slot).start()
            slot = (1 - y) * zs + zz
            copy_a(slot).wait_recv()
            product(1 - y, core, zz, (load_at(a_in, slot),), store_at(b_out, zz))
            copy_b(zz).start()

        run(valid, pair_step)
    for valid, zz, way in rounds[:-1]:
        first = (z == 0) if way == 0 else (z == zs - 1)

        def line_step():
            slot = y * zs + zz
            copy_a(slot).wait_recv()
            copy_b(zz).wait_recv()
            near = (load_at(a_in, slot), load_at(b_in, zz))

            @pl.when(first)
            def _():
                product(y, core, zz, near, store_at(c_out, zz))

            @pl.when(jnp.logical_not(first))
            def _():
                copy_c(way, zz).wait_recv()
                product(y, core, zz, near + (load_at(c_in, way, zz),), store_at(c_out, zz))

            copy_c(way, zz).start()

        run(valid, line_step)
    slot = y * zs + z
    copy_a(slot).wait_recv()
    copy_b(z).wait_recv()

    def finish(cols, acc):
        out_ref[:, cols] = (
            acc + bias_ref[:, cols] - x_ref[:, cols].astype(jnp.float32)
        ).astype(jnp.bfloat16)

    near = (load_at(a_in, slot), load_at(b_in, z))

    @pl.when(z == 0)
    def _():
        copy_c(1, z).wait_recv()
        product(y, core, z, near + (load_at(c_in, 1, z),), finish)

    @pl.when(z == zs - 1)
    def _():
        copy_c(0, z).wait_recv()
        product(y, core, z, near + (load_at(c_in, 0, z),), finish)

    @pl.when((z > 0) & (z < zs - 1))
    def _():
        copy_c(1, z).wait_recv()
        copy_c(0, z).wait_recv()
        product(y, core, z, near + (load_at(c_in, 0, z), load_at(c_in, 1, z)), finish)

    for slot in range(2 * zs):
        copy_a(slot).wait_send()
    for zz in range(zs):
        copy_b(zz).wait_send()
    for valid, zz, way in rounds[:-1]:
        run(valid, lambda: copy_c(way, zz).wait_send())


def reduce_rows(x, bias, codes, dec_weight, collective_id):
    zs = lax.axis_size("feat")
    rows, width = x.shape
    slab = lambda *lead: pltpu.VMEM(lead + (rows, width), jnp.bfloat16)
    sem = lambda *lead: pltpu.SemaphoreType.DMA(lead)
    return pl.pallas_call(
        functools.partial(reduce_kernel, zs),
        out_shape=jax.ShapeDtypeStruct((rows, width), jnp.bfloat16),
        in_specs=[pl.BlockSpec(memory_space=pltpu.VMEM)] * 4,
        out_specs=pl.BlockSpec(memory_space=pltpu.VMEM),
        scratch_shapes=[
            slab(2 * zs), slab(2 * zs), slab(zs), slab(zs), slab(zs), slab(2, zs),
            sem(2 * zs), sem(2 * zs), sem(zs), sem(zs), sem(zs), sem(2, zs),
        ],
        compiler_params=pltpu.CompilerParams(
            collective_id=collective_id, has_side_effects=True, vmem_limit_bytes=48 * 1024 * 1024
        ),
        name="reduce_rows",
    )(x, bias.reshape(1, width), codes, dec_weight)


def gathered_plan(activations, block_lists, top_positions, enc_weight, enc_bias, dec_weight, dec_bias):
    ids = global_ids(block_lists, top_positions, enc_weight.shape[1])
    all_x, code_vals, mask = encode_rows(activations, ids, enc_weight, enc_bias, 1)
    residual = reduce_rows(activations, dec_bias, code_vals, dec_weight, 2)
    enc_turned, dec_grad = gradient_rows(residual, all_x, code_vals, mask, dec_weight, 3)
    return (enc_turned.T, dec_grad)


def on_device(activations, block_lists, top_positions, *weights):
    owner_count = lax.axis_size(GROUP)
    pairs = activations.shape[0] * block_lists.shape[1]
    gathered = owner_count * activations.shape[0]
    square = lax.axis_size("tok") == 4 and activations.shape[1] % 768 == 0
    if square and gathered <= 4 * pairs:
        return gathered_plan(activations, block_lists, top_positions, *weights)
    return routed_plan(activations, block_lists, top_positions, *weights)


def solution(mesh):
    placed = (
        P(("grp", "tok", "feat"), None),
        P(("grp", "tok", "feat"), None),
        P(("grp", "tok", "feat"), None),
        P(None, ("tok", "feat")),
        P(("tok", "feat")),
        P(("tok", "feat"), None),
        P(),
    )
    return jax.shard_map(
        on_device,
        mesh=mesh,
        in_specs=placed,
        out_specs=(P(None, ("grp", "tok", "feat")), P(("grp", "tok", "feat"), None)),
        check_vma=False,
    )
```
